256 devices in a mesh: seq: 32 (over z_hi, x, core), fsdp: 8 (over z_lo, y).
Axes of the slice: x: 4, y: 4, z: 8 (z_hi: 4, z_lo: 2; z = z_hi * 2 + z_lo), core: 2. Of those that a mesh axis runs over, the one named last changes fastest.
Arguments:
- inputs: bfloat16 [8, 128, 32, 4096], P('fsdp', None, 'seq'), may hold values from -6 to 6
- queries: bfloat16 [8, 128, 32, 4096], P('fsdp', None, 'seq'), may hold values from -1000 to 1000
- rotated_keys: bfloat16 [8, 128, 32, 512], P('fsdp', None, 'seq'), may hold values from -6 to 6
- out_grad: bfloat16 [8, 128, 32, 4096], P('fsdp', None, 'seq'), may hold values from -6 to 6
- value_weight: bfloat16 [4096, 512], P(('seq', 'fsdp')), may hold values from -0.09375 to 0.09375
- fisher: float32 [4096, 512], P(('seq', 'fsdp')), may hold values from 0.2 to 20
- anchor: float32 [4096, 512], P(('seq', 'fsdp')), may hold values from -0.25 to 0.25
- doc_starts: int32 [8, 64], P('fsdp'), may hold values from 0 to 4064, as said below
- owners: int32 [8, 64], P('fsdp'), may hold values from 0 to 31, as said below
Outputs:
- query_grad: bfloat16 [8, 32, 6, 32, 4096], P('fsdp', 'seq')
- key_grad: bfloat16 [8, 128, 32, 512], P('fsdp', None, 'seq')
- input_grad: bfloat16 [8, 128, 32, 4096], P('fsdp', None, 'seq')
- ewc_grad: float32 [4096, 512], P(('seq', 'fsdp'))
The draws below stay inside these ranges and needn't reach their ends.
Inputs may be any that keep to these rules, and one draw needn't show every extreme that they name: `doc_starts`: in each sequence the starts rise strictly from 0; every document's length (4096 minus the last start for the last one) is a multiple of 32. Each of the 32 owners is named by exactly two documents of a sequence; one owner's documents hold at most 192 positions in all, and in every sequence some owner holds exactly that many.
All inputs are finite; a program needn't handle non-finite values.
Results may differ from the reference program's by a relative error of at most 0.029.
Values may be sent and summed in bfloat16 or wider, within the bound.
No kernel may reach another device: no remote copies, remote signals or barrier semaphores. Data moves between devices by JAX's collectives and lax.ppermute only.
A program may use at most 128 MiB of HBM per device.

```python
import math
import jax
import jax.numpy as jnp
from jax import lax

D = 4096
HEADS = 32
KVH = 4
HD = 128
TOK_DEV = 128
QW = 4096
KVW = 512
CAP = 6
SEQS = 8
TOKENS = 32768
N_SEQ = 32


def plan_sequence(key):
    lane_count = N_SEQ
    star_key, fill_key, split_key, order_key = jax.random.split(key, 4)
    star = jax.random.randint(star_key, (), 0, lane_count)
    lane_ids = jnp.arange(lane_count, dtype=jnp.int32)
    loads = jnp.where(lane_ids == star, CAP, 2).astype(jnp.int32)
    spare = TOK_DEV - 2 * (lane_count - 1) - CAP

    def add_unit(step_index, current):
        ranking = jax.random.randint(jax.random.fold_in(fill_key, step_index), (lane_count,), 0, 1 << 20) * lane_count + lane_ids
        open_lane = (current < CAP) & (lane_ids != star)
        ranking = jnp.where(open_lane, ranking, -1)
        chosen = jnp.argmax(ranking)
        return current + (lane_ids == chosen).astype(jnp.int32)
    loads = lax.fori_loop(0, spare, add_unit, loads)
    first_part = 1 + jax.random.randint(split_key, (lane_count,), 0, 1 << 20) % (loads - 1)
    doc_lengths = jnp.concatenate([first_part, loads - first_part])
    owner_ids = jnp.concatenate([lane_ids, lane_ids])
    order = jax.random.permutation(order_key, 2 * lane_count)
    doc_lengths = doc_lengths[order]
    owner_ids = owner_ids[order]
    starts = (jnp.cumsum(doc_lengths) - doc_lengths) * lane_count
    return (starts.astype(jnp.int32), owner_ids.astype(jnp.int32))


def plan_all(key):
    seq_keys = jax.random.split(jax.random.fold_in(key, 7), SEQS)
    return jax.vmap(plan_sequence)(seq_keys)


def draw_doc_starts(key, part):
    return plan_all(key)[0]


def draw_owners(key, part):
    return plan_all(key)[1]


def draw_queries(key, part):
    base_key = jax.random.fold_in(jax.random.fold_in(key, 11), 0)
    head_shape = (SEQS, TOK_DEV, N_SEQ, HEADS, HD)
    values = jax.random.normal(base_key, head_shape, jnp.float32)
    values = jnp.clip(values, -1000.0, 1000.0)
    return values.reshape(SEQS, TOK_DEV, N_SEQ, HEADS * HD).astype(jnp.bfloat16)


def level_of(key, shape, pieces, smallest, high):
    level = 1.0
    for axis_at, blocks in pieces:
        draws = jax.random.uniform(jax.random.fold_in(jax.random.fold_in(key, 6), axis_at), (blocks,), jnp.float32, smallest / len(pieces), high / len(pieces))
        level = level * jnp.repeat(jnp.exp(draws), shape[axis_at] // blocks).reshape((-1,) + (1,) * (len(shape) - 1 - axis_at))
    return level


def noise(stream_key, extent, scale, bound, pieces=(), kind=jnp.bfloat16):
    result = jax.random.normal(stream_key, extent, jnp.float32) * scale
    if len(pieces) > 0:
        result = level_of(stream_key, extent, pieces, -0.22, 0.18) * result
    return jnp.clip(result, min=-bound, max=bound).astype(kind)


def setup_inputs(seed: int = 0) -> dict:
    splits = jax.random.split(jax.random.key(seed), 10)
    inputs = noise(splits[0], (SEQS, TOK_DEV, N_SEQ, D), 1.0, 6.0, ((0, 8), (2, 32)))
    queries = draw_queries(jax.random.fold_in(splits[9], 71), 0)
    rotated_keys = noise(splits[2], (SEQS, TOK_DEV, N_SEQ, KVW), 1.0, 6.0, ((0, 8), (2, 32)))
    out_grad = noise(splits[3], (SEQS, TOK_DEV, N_SEQ, QW), 1.0, 6.0, ((0, 8), (2, 32)))
    value_weight = noise(splits[4], (D, KVW), D ** -0.5, 0.09375, ((0, 256),))
    fisher = jnp.clip(jnp.exp(math.log(20.0) - 4.6051702 * jax.random.uniform(splits[5], (D, KVW), jnp.float32) ** level_of(splits[5], (D, KVW), ((0, 256),), -0.2, 0.2)), 0.2, 20.0)
    anchor = noise(splits[6], (D, KVW), 0.015625, 0.25, ((0, 256),), jnp.float32)
    doc_starts = draw_doc_starts(jax.random.fold_in(splits[9], 71), 0)
    owners = draw_owners(jax.random.fold_in(splits[9], 71), 0)
    return dict(inputs=inputs, queries=queries, rotated_keys=rotated_keys, out_grad=out_grad, value_weight=value_weight, fisher=fisher, anchor=anchor, doc_starts=doc_starts, owners=owners)


SCORE_NEG = -1e+30
EWC_LAMBDA = 4.0

def round_plan(starts, owner_list, lane_count, rounds):
    round_ids = jnp.arange(rounds, dtype=jnp.int32)
    start_rounds = starts // lane_count
    doc_of = lax.optimization_barrier(jnp.sum((start_rounds[None, :] <= round_ids[:, None]).astype(jnp.int32), axis=1)) - 1
    doc_ids = jnp.arange(starts.shape[0], dtype=jnp.int32)
    onehot = (doc_of[:, None] == doc_ids[None, :]).astype(jnp.int32)
    owner_of = lax.optimization_barrier(jnp.sum(onehot * owner_list[None, :], axis=1))
    earlier = (owner_of[:, None] == owner_of[None, :]) & (round_ids[None, :] < round_ids[:, None])
    rank_of = lax.optimization_barrier(jnp.sum(earlier.astype(jnp.int32), axis=1))
    return (doc_of, owner_of, rank_of)

def slot_rounds(owner_of, rank_of, lane_count, capacity):
    lane_ids = jnp.arange(lane_count, dtype=jnp.int32)
    slot_ids = jnp.arange(capacity, dtype=jnp.int32)
    round_ids = jnp.arange(owner_of.shape[0], dtype=jnp.int32)
    match = (owner_of[None, None, :] == lane_ids[None, :, None]) & (rank_of[None, None, :] == slot_ids[:, None, None])
    source = lax.optimization_barrier(jnp.sum(match.astype(jnp.int32) * round_ids[None, None, :], axis=2))
    filled = jnp.any(match, axis=2)
    return (source, filled)

def one_sequence(token_in, query_in, key_in, grad_in, starts, owner_list, weight):
    length = TOK_DEV * N_SEQ
    block_rows = 128
    reach = CAP * N_SEQ
    width = block_rows + reach
    group = HEADS // KVH
    scale = 1.0 / math.sqrt(HD)
    token_flat = token_in.reshape(length, D)
    query_flat = query_in.reshape(length, HEADS * HD)
    key_flat = key_in.reshape(length, KVH * HD)
    grad_flat = grad_in.reshape(length, HEADS * HD)
    value_flat = jnp.dot(token_flat, weight, preferred_element_type=jnp.float32).astype(jnp.bfloat16)
    positions = jnp.arange(length, dtype=jnp.int32)
    doc_pos = lax.optimization_barrier(jnp.sum((starts[None, :] <= positions[:, None]).astype(jnp.int32), axis=1)) - 1

    def step(carry, block):
        key_acc, value_acc = carry
        q_start = (block * block_rows).astype(jnp.int32)
        k_start = jnp.maximum(q_start - reach, 0).astype(jnp.int32)
        q_blk = lax.dynamic_slice_in_dim(query_flat, q_start, block_rows, 0).reshape(block_rows, KVH, group, HD).astype(jnp.float32)
        g_blk = lax.dynamic_slice_in_dim(grad_flat, q_start, block_rows, 0).reshape(block_rows, KVH, group, HD).astype(jnp.float32)
        k_blk = lax.dynamic_slice_in_dim(key_flat, k_start, width, 0).reshape(width, KVH, HD).astype(jnp.float32)
        v_blk = lax.dynamic_slice_in_dim(value_flat, k_start, width, 0).reshape(width, KVH, HD).astype(jnp.float32)
        q_doc = lax.dynamic_slice_in_dim(doc_pos, q_start, block_rows, 0)
        k_doc = lax.dynamic_slice_in_dim(doc_pos, k_start, width, 0)
        q_pos = q_start + jnp.arange(block_rows, dtype=jnp.int32)
        k_pos = k_start + jnp.arange(width, dtype=jnp.int32)
        visible = (q_doc[:, None] == k_doc[None, :]) & (k_pos[None, :] <= q_pos[:, None])
        scores = jnp.einsum('qhgd,khd->hgqk', q_blk, k_blk) * scale
        masked = jnp.where(visible, scores, SCORE_NEG)
        peak = lax.optimization_barrier(jnp.max(masked, axis=3, keepdims=True))
        probs = jnp.where(visible, jnp.exp(masked - peak), 0.0)
        probs = probs / lax.optimization_barrier(jnp.sum(probs, axis=3, keepdims=True))
        probs_b = lax.optimization_barrier(probs.astype(jnp.bfloat16)).astype(jnp.float32)
        attn_out = jnp.einsum('hgqk,khd->qhgd', probs_b, v_blk)
        attn_out = lax.optimization_barrier(attn_out.astype(jnp.bfloat16)).astype(jnp.float32)
        delta = jnp.einsum('qhgd,qhgd->hgq', g_blk, attn_out)
        dprobs = jnp.einsum('qhgd,khd->hgqk', g_blk, v_blk)
        dscores = probs * (dprobs - delta[..., None]) * scale
        dscores = lax.optimization_barrier(dscores.astype(jnp.bfloat16)).astype(jnp.float32)
        query_part = jnp.einsum('hgqk,khd->qhgd', dscores, k_blk).astype(jnp.bfloat16).reshape(block_rows, HEADS * HD)
        key_part = jnp.einsum('hgqk,qhgd->khd', dscores, q_blk).reshape(width, KVH * HD)
        value_part = jnp.einsum('hgqk,qhgd->khd', probs_b, g_blk).reshape(width, KVH * HD)
        key_acc = lax.dynamic_update_slice_in_dim(key_acc, lax.dynamic_slice_in_dim(key_acc, k_start, width, 0) + key_part, k_start, 0)
        value_acc = lax.dynamic_update_slice_in_dim(value_acc, lax.dynamic_slice_in_dim(value_acc, k_start, width, 0) + value_part, k_start, 0)
        return ((key_acc, value_acc), query_part)
    blocks = jnp.arange(length // block_rows, dtype=jnp.int32)
    zeros_kv = jnp.zeros((length, KVH * HD), jnp.float32)
    (key_acc, value_acc), query_parts = lax.scan(step, (zeros_kv, zeros_kv), blocks)
    query_home = query_parts.reshape(length, HEADS * HD)
    key_grad = key_acc.astype(jnp.bfloat16)
    value_grad = value_acc.astype(jnp.bfloat16)
    input_grad = jnp.dot(value_grad, weight.T, preferred_element_type=jnp.float32).astype(jnp.bfloat16)
    partial_sum = jnp.dot(token_flat.T, value_grad, preferred_element_type=jnp.float32)
    doc_of, owner_of, rank_of = round_plan(starts, owner_list, N_SEQ, TOK_DEV)
    source, filled = slot_rounds(owner_of, rank_of, N_SEQ, CAP)
    query_rounds = query_home.reshape(TOK_DEV, N_SEQ, HEADS * HD)
    picked = jnp.take(query_rounds, source.T.reshape(-1), axis=0).reshape(N_SEQ, CAP, N_SEQ, HEADS * HD)
    query_slots = jnp.where(filled.T[:, :, None, None], picked, jnp.zeros_like(picked))
    return (query_slots, key_grad.reshape(TOK_DEV, N_SEQ, KVH * HD), input_grad.reshape(TOK_DEV, N_SEQ, D), partial_sum)

def reference(inputs, queries, rotated_keys, out_grad, value_weight, fisher, anchor, doc_starts, owners):

    def per_sequence(carry, index):
        results = one_sequence(inputs[index], queries[index], rotated_keys[index], out_grad[index], doc_starts[index], owners[index], value_weight)
        return (carry + results[3], (results[0], results[1], results[2]))
    seq_ids = jnp.arange(SEQS, dtype=jnp.int32)
    weight_sum, outs = lax.scan(per_sequence, jnp.zeros((D, KVH * HD), jnp.float32), seq_ids)
    grad_scale = 1.0 / math.sqrt(TOKENS)
    ewc_grad = weight_sum * grad_scale + EWC_LAMBDA * fisher * (value_weight.astype(jnp.float32) - anchor)
    return (outs[0], outs[1], outs[2], ewc_grad)
```

```python
import math

import jax
import jax.numpy as jnp
from jax import lax
from jax.experimental import pallas as pl
from jax.experimental.pallas import tpu as pltpu
from jax.sharding import PartitionSpec as P


KVH = 4
HD = 128
GROUP = 8
LANES = 32
PEERS = 8
CAP = 6
CAP8 = 8
ROUNDS = 128
WROWS = 16
HROWS = CAP * GROUP
MROWS = HROWS + WROWS + CAP8
ROWS = LANES * HROWS
KEYS = LANES * CAP8
CHUNKS = 6
CHUNK = ROWS // CHUNKS
SCORE_NEG = -1e30
EWC_LAMBDA = 4.0
SCALE = 1.0 / math.sqrt(HD)
BF = jnp.bfloat16
F32 = jnp.float32


def exchange(value, axes):
    return lax.all_to_all(value, axes, split_axis=0, concat_axis=0, tiled=True)


def round_plan(starts, owner_list):
    round_ids = jnp.arange(ROUNDS, dtype=jnp.int32)
    start_rounds = starts // LANES
    doc_of = jnp.sum((start_rounds[None, :] <= round_ids[:, None]).astype(jnp.int32), axis=1) - 1
    doc_ids = jnp.arange(starts.shape[0], dtype=jnp.int32)
    onehot = (doc_of[:, None] == doc_ids[None, :]).astype(jnp.int32)
    owner_of = jnp.sum(onehot * owner_list[None, :], axis=1)
    earlier = (owner_of[:, None] == owner_of[None, :]) & (round_ids[None, :] < round_ids[:, None])
    rank_of = jnp.sum(earlier.astype(jnp.int32), axis=1)
    return doc_of, owner_of, rank_of


def pick_rows(code, count):
    slots = lax.broadcasted_iota(jnp.int32, (count, ROUNDS), 0)
    return (slots == code).astype(F32).astype(BF)


def spread_heads(code, x_ref, acc_ref):
    rows = jnp.dot(pick_rows(code, CAP * LANES), x_ref[...], preferred_element_type=F32)
    for g in range(GROUP):
        for s in range(CAP):
            acc_ref[pl.ds(s * GROUP + g, LANES, stride=HROWS), :] = rows[
                s * LANES : (s + 1) * LANES, g * HD : (g + 1) * HD
            ]
    return acc_ref[...].astype(BF).reshape(LANES, HROWS, HD)


def pack_grad_kernel(code_ref, g_ref, out_ref, acc_ref):
    out_ref[:, 0] = spread_heads(code_ref[0:1, :], g_ref, acc_ref)


def pack_query_kernel(code_ref, q_ref, k_ref, w_ref, out_ref, acc_ref):
    out_ref[:, 0, 0:HROWS] = spread_heads(code_ref[0:1, :], q_ref, acc_ref)
    out_ref[:, 0, HROWS : HROWS + WROWS] = jnp.broadcast_to(w_ref[...][None], (LANES, WROWS, HD))
    keys = jnp.dot(pick_rows(code_ref[1:2, :], KEYS), k_ref[...], preferred_element_type=F32)
    out_ref[:, 0, HROWS + WROWS :] = keys.reshape(LANES, CAP8, HD).astype(BF)


def code_spec():
    return pl.BlockSpec((2, ROUNDS), lambda h: (0, 0))


def head_spec(rows):
    return pl.BlockSpec((LANES, 1, rows, HD), lambda h: (0, h, 0, 0))


def key_spec():
    return pl.BlockSpec((LANES, CAP8, HD), lambda h: (0, 0, h))


def probs_spec():
    return pl.BlockSpec((1, ROWS, KEYS), lambda h: (h, 0, 0))


def pack_query(codes, queries, keys, weight):
    return pl.pallas_call(
        pack_query_kernel,
        grid=(KVH,),
        in_specs=[
            code_spec(),
            pl.BlockSpec((ROUNDS, GROUP * HD), lambda h: (0, h)),
            pl.BlockSpec((ROUNDS, HD), lambda h: (0, h)),
            pl.BlockSpec((WROWS, HD), lambda h: (0, h)),
        ],
        out_specs=head_spec(MROWS),
        out_shape=jax.ShapeDtypeStruct((LANES, KVH, MROWS, HD), BF),
        scratch_shapes=[pltpu.VMEM((ROWS, HD), F32)],
        name="pack_query",
    )(codes, queries, keys, weight)


def pack_grad(codes, grads):
    return pl.pallas_call(
        pack_grad_kernel,
        grid=(KVH,),
        in_specs=[code_spec(), pl.BlockSpec((ROUNDS, GROUP * HD), lambda h: (0, h))],
        out_specs=head_spec(HROWS),
        out_shape=jax.ShapeDtypeStruct((LANES, KVH, HROWS, HD), BF),
        scratch_shapes=[pltpu.VMEM((ROWS, HD), F32)],
        name="pack_grad",
    )(codes, grads)


def mix_matrix(turned):
    a = lax.broadcasted_iota(jnp.int32, (1024, 1024), 1 if turned else 0)
    b = lax.broadcasted_iota(jnp.int32, (1024, 1024), 0 if turned else 1)
    target = ((a >> 4) & 7) * 128 + (a >> 7) * 16 + (a & 15)
    return (target == b).astype(F32).astype(BF)


def split_kernel(x_ref, out_ref, mix_ref):
    @pl.when(pl.program_id(0) == 0)
    def _():
        mix_ref[...] = mix_matrix(False)

    mixed = jnp.dot(x_ref[...], mix_ref[...], preferred_element_type=F32)
    for f in range(PEERS):
        out_ref[f] = mixed[:, f * 128 : (f + 1) * 128].astype(BF)


def split_features(rows):
    return pl.pallas_call(
        split_kernel,
        grid=(4,),
        in_specs=[pl.BlockSpec((ROUNDS, 1024), lambda q: (0, q))],
        out_specs=pl.BlockSpec((PEERS, ROUNDS, 128), lambda q: (0, 0, q)),
        out_shape=jax.ShapeDtypeStruct((PEERS, ROUNDS, 512), BF),
        scratch_shapes=[pltpu.VMEM((1024, 1024), BF)],
        name="split_features",
    )(rows)


def join_kernel(x_ref, out_ref, mix_ref):
    @pl.when(pl.program_id(0) == 0)
    def _():
        mix_ref[...] = mix_matrix(True)

    parts = jnp.concatenate([x_ref[f] for f in range(PEERS)], axis=1)
    out_ref[...] = jnp.dot(parts, mix_ref[...], preferred_element_type=F32).astype(BF)


def join_features(parts):
    return pl.pallas_call(
        join_kernel,
        grid=(4,),
        in_specs=[pl.BlockSpec((PEERS, ROUNDS, 128), lambda q: (0, 0, q))],
        out_specs=pl.BlockSpec((ROUNDS, 1024), lambda q: (0, q)),
        out_shape=jax.ShapeDtypeStruct((ROUNDS, 4096), BF),
        scratch_shapes=[pltpu.VMEM((1024, 1024), BF)],
        name="join_features",
    )(parts)


def doc_table(slot, doc_ref):
    table = jnp.full(slot.shape, -2, jnp.int32)
    for s in range(CAP):
        table = jnp.where(slot == s, doc_ref[s], table)
    return table


def own_keys(block_ref):
    return block_ref[:, 0, HROWS + WROWS :].astype(F32).reshape(KEYS, HD).astype(BF)


def probs_kernel(doc_ref, own_ref, p_ref, bias_ref):
    @pl.when(pl.program_id(0) == 0)
    def _():
        shape = (LANES, HROWS, KEYS)
        q_lane = lax.broadcasted_iota(jnp.int32, shape, 0)
        q_slot = lax.broadcasted_iota(jnp.int32, shape, 1) >> 3
        key = lax.broadcasted_iota(jnp.int32, shape, 2)
        k_lane = key >> 3
        k_slot = key & 7
        seen = (doc_table(q_slot, doc_ref) == doc_table(k_slot, doc_ref)) & (
            k_slot * LANES + k_lane <= q_slot * LANES + q_lane
        )
        bias_ref[...] = jnp.where(seen, 0.0, SCORE_NEG).astype(F32).reshape(ROWS, KEYS)

    query = own_ref[:, 0, 0:HROWS].reshape(ROWS, HD)
    keys = own_keys(own_ref)
    for c in range(CHUNKS):
        rows = slice(c * CHUNK, (c + 1) * CHUNK)
        scores = lax.dot_general(
            query[rows], keys, (((1,), (1,)), ((), ())), preferred_element_type=F32
        )
        scores = scores * SCALE + bias_ref[rows, :]
        peak = jnp.max(scores, axis=1, keepdims=True)
        weight = jnp.exp(scores - peak)
        total = jnp.sum(weight, axis=1, keepdims=True)
        p_ref[0, rows, :] = (weight * (1.0 / total)).astype(BF)


def attend_probs(slot_doc, own):
    return pl.pallas_call(
        probs_kernel,
        grid=(KVH,),
        in_specs=[pl.BlockSpec(memory_space=pltpu.SMEM), head_spec(MROWS)],
        out_specs=probs_spec(),
        out_shape=jax.ShapeDtypeStruct((KVH, ROWS, KEYS), BF),
        scratch_shapes=[pltpu.VMEM((ROWS, KEYS), F32)],
        name="attend_probs",
    )(slot_doc, own)


def value_kernel(p_ref, g_ref, dv_ref):
    grad = g_ref[...].reshape(ROWS, HD)
    turned = lax.dot_general(
        grad, p_ref[0], (((0,), (0,)), ((), ())), preferred_element_type=F32
    )
    dv_ref[...] = turned.T.astype(BF).reshape(LANES, CAP8, HD)


def attend_value(probs, grad):
    return pl.pallas_call(
        value_kernel,
        grid=(KVH,),
        in_specs=[probs_spec(), head_spec(HROWS)],
        out_specs=key_spec(),
        out_shape=jax.ShapeDtypeStruct((LANES, CAP8, KVH * HD), BF),
        name="attend_value",
    )(probs, grad)


def query_kernel(p_ref, own_ref, g_ref, v_ref, dq_ref, dk_ref, ds_ref, acc_ref):
    query = own_ref[:, 0, 0:HROWS].reshape(ROWS, HD)
    keys = own_keys(own_ref)
    grad = g_ref[...].reshape(ROWS, HD)
    values = v_ref[...].astype(F32).reshape(KEYS, HD).astype(BF)
    for c in range(CHUNKS):
        rows = slice(c * CHUNK, (c + 1) * CHUNK)
        probs = p_ref[0, rows, :]
        grad_c = grad[rows]
        attn = jnp.dot(probs, values, preferred_element_type=F32).astype(BF)
        delta = jnp.sum(grad_c.astype(F32) * attn.astype(F32), axis=1, keepdims=True)
        dprobs = lax.dot_general(
            grad_c, values, (((1,), (1,)), ((), ())), preferred_element_type=F32
        )
        dscores = (probs.astype(F32) * (dprobs - delta) * SCALE).astype(BF)
        ds_ref[rows, :] = dscores
        acc_ref[rows, :] = jnp.dot(dscores, keys, preferred_element_type=F32)
    for g in range(GROUP):
        for s in range(CAP):
            dq_ref[s, :, g * HD : (g + 1) * HD] = acc_ref[
                pl.ds(s * GROUP + g, LANES, stride=HROWS), :
            ].astype(BF)
    turned = lax.dot_general(
        query, ds_ref[...], (((0,), (0,)), ((), ())), preferred_element_type=F32
    )
    dk_ref[...] = turned.T.astype(BF).reshape(LANES, CAP8, HD)


def attend_query(probs, own, grad, values):
    return pl.pallas_call(
        query_kernel,
        grid=(KVH,),
        in_specs=[probs_spec(), head_spec(MROWS), head_spec(HROWS), key_spec()],
        out_specs=(pl.BlockSpec((CAP, LANES, GROUP * HD), lambda h: (0, 0, h)), key_spec()),
        out_shape=(
            jax.ShapeDtypeStruct((CAP, LANES, KVH * GROUP * HD), BF),
            jax.ShapeDtypeStruct((LANES, CAP8, KVH * HD), BF),
        ),
        scratch_shapes=[pltpu.VMEM((ROWS, KEYS), BF), pltpu.VMEM((ROWS, HD), F32)],
        name="attend_query",
    )(probs, own, grad, values)


def body(inputs, queries, rotated_keys, out_grad, value_weight, fisher, anchor, doc_starts, owners):
    own_lane = lax.axis_index("seq")
    token_rows = inputs.reshape(ROUNDS, -1)
    query_rows = queries.reshape(ROUNDS, -1)
    key_rows = rotated_keys.reshape(ROUNDS, -1)
    grad_rows = out_grad.reshape(ROUNDS, -1)
    doc_of, owner_of, rank_of = round_plan(doc_starts[0], owners[0])
    home_code = owner_of * CAP8 + rank_of
    codes = jnp.stack([rank_of * LANES + owner_of, home_code])
    slot_ids = jnp.arange(CAP8, dtype=jnp.int32)
    mine = (owner_of[None, :] == own_lane) & (rank_of[None, :] == slot_ids[:, None])
    slot_doc = jnp.sum(jnp.where(mine, doc_of[None, :] + 1, 0), axis=1) - 1
    pick = (jnp.arange(KEYS, dtype=jnp.int32)[:, None] == home_code[None, :]).astype(BF)

    def place(rows):
        return jnp.dot(pick, rows, preferred_element_type=F32).astype(BF).reshape(LANES, CAP8, -1)

    def collect(slots):
        return lax.dot_general(
            pick, slots.reshape(KEYS, -1), (((0,), (0,)), ((), ())), preferred_element_type=F32
        ).astype(BF)

    own = exchange(pack_query(codes, query_rows, key_rows, value_weight), "seq")
    token_split = split_features(token_rows)
    grad_split = pack_grad(codes, grad_rows)
    token_split, own = lax.optimization_barrier((token_split, own))
    token_part = exchange(token_split, "fsdp").reshape(PEERS * ROUNDS, -1)
    probs = attend_probs(slot_doc, own)
    weight_part = own[:, :, HROWS : HROWS + WROWS].transpose(0, 2, 1, 3).reshape(LANES * WROWS, -1)
    grad_split, token_part = lax.optimization_barrier((grad_split, token_part))
    grad_own = exchange(grad_split, "seq")
    value_part = jnp.dot(token_part, weight_part, preferred_element_type=F32).astype(BF)
    value_part, grad_own = lax.optimization_barrier((value_part, grad_own))
    value_parts = exchange(value_part.reshape(PEERS, ROUNDS, -1), "fsdp")
    value_back = attend_value(probs, grad_own)
    values = jnp.sum(value_parts.astype(F32), axis=0).astype(BF)

    both = exchange(jnp.concatenate([place(values), value_back], axis=1), "seq")
    value_home = collect(both[:, CAP8:])
    value_all = exchange(
        jnp.broadcast_to(value_home[None], (PEERS,) + value_home.shape), "fsdp"
    ).reshape(PEERS * ROUNDS, -1)
    query_out, key_back = attend_query(probs, own, grad_own, both)

    input_part = lax.dot_general(
        value_all, weight_part, (((1,), (1,)), ((), ())), preferred_element_type=F32
    ).astype(BF)
    input_parts = exchange(input_part.reshape(PEERS, ROUNDS, -1), "fsdp")
    weight_grad = lax.dot_general(
        token_part, value_all, (((0,), (0,)), ((), ())), preferred_element_type=F32
    ).astype(BF)
    back = jnp.concatenate([weight_grad.reshape(LANES, WROWS, -1), key_back], axis=1)
    back, input_parts = lax.optimization_barrier((back, input_parts))
    last = exchange(back, "seq")
    input_grad = join_features(input_parts)
    weight_sum = jnp.sum(last[:, :WROWS].astype(F32), axis=0)
    key_home = collect(last[:, WROWS:])

    tokens_total = ROUNDS * LANES * PEERS
    ewc_grad = weight_sum * (1.0 / math.sqrt(tokens_total)) + EWC_LAMBDA * fisher * (
        value_weight.astype(F32) - anchor
    )
    return (
        query_out.reshape(1, 1, CAP, LANES, -1),
        key_home.reshape(1, ROUNDS, 1, -1),
        input_grad.reshape(1, ROUNDS, 1, -1),
        ewc_grad,
    )


def solution(mesh):
    rows = P("fsdp", None, "seq", None)
    weights = P(("seq", "fsdp"), None)
    plan = P("fsdp", None)
    return jax.shard_map(
        body,
        mesh=mesh,
        in_specs=(rows, rows, rows, rows, weights, weights, weights, plan, plan),
        out_specs=(P("fsdp", "seq", None, None, None), rows, rows, weights),
        check_vma=False,
    )
```

```python
import math

import jax
import jax.numpy as jnp
from jax import lax
from jax.experimental import pallas as pl
from jax.experimental.pallas import tpu as pltpu
from jax.sharding import Mesh, PartitionSpec as P


KVH = 4
HD = 128
GROUP = 8
LANES = 32
PEERS = 8
FEATS = 512
RING = 4
FEAT = ("zl", "y")
SEQ = ("zh", "x", "core")
CAP = 6
CAP8 = 8
ROUNDS = 128
WROWS = 16
HROWS = CAP * GROUP
MROWS = HROWS + CAP8
ROWS = LANES * HROWS
KEYS = LANES * CAP8
CHUNKS = 6
CHUNK = ROWS // CHUNKS
SCORE_NEG = -1e30
EWC_LAMBDA = 4.0
SCALE = 1.0 / math.sqrt(HD)
BF = jnp.bfloat16
F32 = jnp.float32


def exchange(value, axes):
    return lax.all_to_all(value, axes, split_axis=0, concat_axis=0, tiled=True)


def round_plan(starts, owner_list):
    round_ids = jnp.arange(ROUNDS, dtype=jnp.int32)
    start_rounds = starts // LANES
    doc_of = jnp.sum((start_rounds[None, :] <= round_ids[:, None]).astype(jnp.int32), axis=1) - 1
    doc_ids = jnp.arange(starts.shape[0], dtype=jnp.int32)
    onehot = (doc_of[:, None] == doc_ids[None, :]).astype(jnp.int32)
    owner_of = jnp.sum(onehot * owner_list[None, :], axis=1)
    earlier = (owner_of[:, None] == owner_of[None, :]) & (round_ids[None, :] < round_ids[:, None])
    rank_of = jnp.sum(earlier.astype(jnp.int32), axis=1)
    return doc_of, owner_of, rank_of


def pick_rows(code, count):
    slots = lax.broadcasted_iota(jnp.int32, (count, ROUNDS), 0)
    return (slots == code).astype(F32).astype(BF)


def spread_heads(code, x_ref, acc_ref):
    rows = jnp.dot(pick_rows(code, CAP * LANES), x_ref[...], preferred_element_type=F32)
    for g in range(GROUP):
        for s in range(CAP):
            acc_ref[pl.ds(s * GROUP + g, LANES, stride=HROWS), :] = rows[
                s * LANES : (s + 1) * LANES, g * HD : (g + 1) * HD
            ]
    return acc_ref[...].astype(BF).reshape(LANES, HROWS, HD)


def pack_grad_kernel(code_ref, g_ref, out_ref, acc_ref):
    out_ref[:, 0] = spread_heads(code_ref[0:1, :], g_ref, acc_ref)


def pack_query_kernel(code_ref, q_ref, k_ref, out_ref, acc_ref):
    out_ref[:, 0, 0:HROWS] = spread_heads(code_ref[0:1, :], q_ref, acc_ref)
    keys = jnp.dot(pick_rows(code_ref[1:2, :], KEYS), k_ref[...], preferred_element_type=F32)
    out_ref[:, 0, HROWS:] = keys.reshape(LANES, CAP8, HD).astype(BF)


def code_spec():
    return pl.BlockSpec((2, ROUNDS), lambda h: (0, 0))


def head_spec(rows):
    return pl.BlockSpec((LANES, 1, rows, HD), lambda h: (0, h, 0, 0))


def key_spec():
    return pl.BlockSpec((LANES, CAP8, HD), lambda h: (0, 0, h))


def probs_spec():
    return pl.BlockSpec((1, ROWS, KEYS), lambda h: (h, 0, 0))


def pack_query(codes, queries, keys):
    return pl.pallas_call(
        pack_query_kernel,
        grid=(KVH,),
        in_specs=[
            code_spec(),
            pl.BlockSpec((ROUNDS, GROUP * HD), lambda h: (0, h)),
            pl.BlockSpec((ROUNDS, HD), lambda h: (0, h)),
        ],
        out_specs=head_spec(MROWS),
        out_shape=jax.ShapeDtypeStruct((LANES, KVH, MROWS, HD), BF),
        scratch_shapes=[pltpu.VMEM((ROWS, HD), F32)],
        name="pack_query",
    )(codes, queries, keys)


def pack_grad(codes, grads):
    return pl.pallas_call(
        pack_grad_kernel,
        grid=(KVH,),
        in_specs=[code_spec(), pl.BlockSpec((ROUNDS, GROUP * HD), lambda h: (0, h))],
        out_specs=head_spec(HROWS),
        out_shape=jax.ShapeDtypeStruct((LANES, KVH, HROWS, HD), BF),
        scratch_shapes=[pltpu.VMEM((ROWS, HD), F32)],
        name="pack_grad",
    )(codes, grads)


def mix_matrix(turned):
    a = lax.broadcasted_iota(jnp.int32, (1024, 1024), 1 if turned else 0)
    b = lax.broadcasted_iota(jnp.int32, (1024, 1024), 0 if turned else 1)
    target = ((a >> 4) & 7) * 128 + (a >> 7) * 16 + (a & 15)
    return (target == b).astype(F32).astype(BF)


def split_kernel(x_ref, out_ref, mix_ref):
    @pl.when(pl.program_id(0) == 0)
    def _():
        mix_ref[...] = mix_matrix(False)

    mixed = jnp.dot(x_ref[...], mix_ref[...], preferred_element_type=F32)
    for f in range(PEERS):
        out_ref[f] = mixed[:, f * 128 : (f + 1) * 128].astype(BF)


def split_features(rows):
    return pl.pallas_call(
        split_kernel,
        grid=(4,),
        in_specs=[pl.BlockSpec((ROUNDS, 1024), lambda q: (0, q))],
        out_specs=pl.BlockSpec((PEERS, ROUNDS, 128), lambda q: (0, 0, q)),
        out_shape=jax.ShapeDtypeStruct((PEERS, ROUNDS, FEATS), BF),
        scratch_shapes=[pltpu.VMEM((1024, 1024), BF)],
        name="split_features",
    )(rows)


def smem():
    return pl.BlockSpec(memory_space=pltpu.SMEM)


def weight_kernel(where_ref, same_ref, other_ref, out_ref):
    core = where_ref[4]
    for x in range(4):
        for z in range(8):
            spot = (z // 2) * 8 + where_ref[x] * 2
            out_ref[z % 2, spot + core] = same_ref[x, z]
            out_ref[z % 2, spot + 1 - core] = other_ref[x, z]


def weight_rows(where, same, other):
    return pl.pallas_call(
        weight_kernel,
        in_specs=[smem()] + [pl.BlockSpec(memory_space=pltpu.VMEM)] * 2,
        out_specs=pl.BlockSpec(memory_space=pltpu.VMEM),
        out_shape=jax.ShapeDtypeStruct((2, LANES, WROWS, KVH * HD), BF),
        name="weight_rows",
    )(where, same, other)


def values_kernel(peer_ref, x_ref, *refs):
    out_ref = refs[RING]
    total = jnp.zeros((ROUNDS, KVH * HD), F32)
    for j in range(RING):
        for z in range(2):
            total = total + jnp.dot(
                x_ref[z * RING + peer_ref[j]], refs[j][z], preferred_element_type=F32
            )
    out_ref[...] = total.astype(BF)


def make_values(peers, split, parts):
    return pl.pallas_call(
        values_kernel,
        in_specs=[smem()] + [pl.BlockSpec(memory_space=pltpu.VMEM)] * (1 + RING),
        out_specs=pl.BlockSpec(memory_space=pltpu.VMEM),
        out_shape=jax.ShapeDtypeStruct((ROUNDS, KVH * HD), BF),
        name="make_values",
    )(peers, split, *parts)


def input_kernel(peer_ref, dv_ref, *refs):
    out_ref, mix_ref, row_ref = refs[RING:]

    @pl.when(pl.program_id(0) == 0)
    def _():
        mix_ref[...] = mix_matrix(True)

    for j in range(RING):
        for z in range(2):
            part = lax.dot_general(
                dv_ref[...], refs[j][z], (((1,), (1,)), ((), ())), preferred_element_type=F32
            )
            lane = pl.multiple_of((z * RING + peer_ref[j]) * 128, 128)
            row_ref[:, pl.ds(lane, 128)] = part.astype(BF)
    out_ref[...] = jnp.dot(row_ref[...], mix_ref[...], preferred_element_type=F32).astype(BF)


def make_input(peers, value_home, parts):
    return pl.pallas_call(
        input_kernel,
        grid=(4,),
        in_specs=[smem(), pl.BlockSpec((ROUNDS, KVH * HD), lambda q: (0, 0))]
        + [pl.BlockSpec((2, 128, KVH * HD), lambda q: (0, q, 0))] * RING,
        out_specs=pl.BlockSpec((ROUNDS, 1024), lambda q: (0, q)),
        out_shape=jax.ShapeDtypeStruct((ROUNDS, 4096), BF),
        scratch_shapes=[pltpu.VMEM((1024, 1024), BF), pltpu.VMEM((ROUNDS, 1024), BF)],
        name="make_input",
    )(peers, value_home, *parts)


def token_kernel(source_ref, *refs):
    out_ref = refs[PEERS]
    for j in range(PEERS):
        out_ref[source_ref[j]] = refs[j][...]


def token_rows_of(sources, parts):
    return pl.pallas_call(
        token_kernel,
        in_specs=[smem()] + [pl.BlockSpec(memory_space=pltpu.VMEM)] * PEERS,
        out_specs=pl.BlockSpec(memory_space=pltpu.VMEM),
        out_shape=jax.ShapeDtypeStruct((PEERS, ROUNDS, FEATS), BF),
        name="token_rows_of",
    )(sources, *parts)


def doc_table(slot, doc_ref):
    table = jnp.full(slot.shape, -2, jnp.int32)
    for s in range(CAP):
        table = jnp.where(slot == s, doc_ref[s], table)
    return table


def own_keys(block_ref):
    return block_ref[:, 0, HROWS:].astype(F32).reshape(KEYS, HD).astype(BF)


def probs_kernel(doc_ref, own_ref, p_ref, bias_ref):
    @pl.when(pl.program_id(0) == 0)
    def _():
        shape = (LANES, HROWS, KEYS)
        q_lane = lax.broadcasted_iota(jnp.int32, shape, 0)
        q_slot = lax.broadcasted_iota(jnp.int32, shape, 1) >> 3
        key = lax.broadcasted_iota(jnp.int32, shape, 2)
        k_lane = key >> 3
        k_slot = key & 7
        seen = (doc_table(q_slot, doc_ref) == doc_table(k_slot, doc_ref)) & (
            k_slot * LANES + k_lane <= q_slot * LANES + q_lane
        )
        bias_ref[...] = jnp.where(seen, 0.0, SCORE_NEG).astype(F32).reshape(ROWS, KEYS)

    query = own_ref[:, 0, 0:HROWS].reshape(ROWS, HD)
    keys = own_keys(own_ref)
    for c in range(CHUNKS):
        rows = slice(c * CHUNK, (c + 1) * CHUNK)
        scores = lax.dot_general(
            query[rows], keys, (((1,), (1,)), ((), ())), preferred_element_type=F32
        )
        scores = scores * SCALE + bias_ref[rows, :]
        peak = jnp.max(scores, axis=1, keepdims=True)
        weight = jnp.exp(scores - peak)
        total = jnp.sum(weight, axis=1, keepdims=True)
        p_ref[0, rows, :] = (weight * (1.0 / total)).astype(BF)


def attend_probs(slot_doc, own):
    return pl.pallas_call(
        probs_kernel,
        grid=(KVH,),
        in_specs=[pl.BlockSpec(memory_space=pltpu.SMEM), head_spec(MROWS)],
        out_specs=probs_spec(),
        out_shape=jax.ShapeDtypeStruct((KVH, ROWS, KEYS), BF),
        scratch_shapes=[pltpu.VMEM((ROWS, KEYS), F32)],
        name="attend_probs",
    )(slot_doc, own)


def value_kernel(p_ref, g_ref, dv_ref):
    grad = g_ref[...].reshape(ROWS, HD)
    turned = lax.dot_general(
        grad, p_ref[0], (((0,), (0,)), ((), ())), preferred_element_type=F32
    )
    dv_ref[...] = turned.T.astype(BF).reshape(LANES, CAP8, HD)


def attend_value(probs, grad):
    return pl.pallas_call(
        value_kernel,
        grid=(KVH,),
        in_specs=[probs_spec(), head_spec(HROWS)],
        out_specs=key_spec(),
        out_shape=jax.ShapeDtypeStruct((LANES, CAP8, KVH * HD), BF),
        name="attend_value",
    )(probs, grad)


def query_kernel(p_ref, own_ref, g_ref, v_ref, dq_ref, dk_ref, ds_ref, acc_ref):
    query = own_ref[:, 0, 0:HROWS].reshape(ROWS, HD)
    keys = own_keys(own_ref)
    grad = g_ref[...].reshape(ROWS, HD)
    values = v_ref[...].astype(F32).reshape(KEYS, HD).astype(BF)
    for c in range(CHUNKS):
        rows = slice(c * CHUNK, (c + 1) * CHUNK)
        probs = p_ref[0, rows, :]
        grad_c = grad[rows]
        attn = jnp.dot(probs, values, preferred_element_type=F32).astype(BF)
        delta = jnp.sum(grad_c.astype(F32) * attn.astype(F32), axis=1, keepdims=True)
        dprobs = lax.dot_general(
            grad_c, values, (((1,), (1,)), ((), ())), preferred_element_type=F32
        )
        dscores = (probs.astype(F32) * (dprobs - delta) * SCALE).astype(BF)
        ds_ref[rows, :] = dscores
        acc_ref[rows, :] = jnp.dot(dscores, keys, preferred_element_type=F32)
    for g in range(GROUP):
        for s in range(CAP):
            dq_ref[s, :, g * HD : (g + 1) * HD] = acc_ref[
                pl.ds(s * GROUP + g, LANES, stride=HROWS), :
            ].astype(BF)
    turned = lax.dot_general(
        query, ds_ref[...], (((0,), (0,)), ((), ())), preferred_element_type=F32
    )
    dk_ref[...] = turned.T.astype(BF).reshape(LANES, CAP8, HD)


def attend_query(probs, own, grad, values):
    return pl.pallas_call(
        query_kernel,
        grid=(KVH,),
        in_specs=[probs_spec(), head_spec(MROWS), head_spec(HROWS), key_spec()],
        out_specs=(pl.BlockSpec((CAP, LANES, GROUP * HD), lambda h: (0, 0, h)), key_spec()),
        out_shape=(
            jax.ShapeDtypeStruct((CAP, LANES, KVH * GROUP * HD), BF),
            jax.ShapeDtypeStruct((LANES, CAP8, KVH * HD), BF),
        ),
        scratch_shapes=[pltpu.VMEM((ROWS, KEYS), BF), pltpu.VMEM((ROWS, HD), F32)],
        name="attend_query",
    )(probs, own, grad, values)


def body(inputs, queries, rotated_keys, out_grad, value_weight, fisher, anchor, doc_starts, owners):
    own_lane = lax.axis_index(SEQ)
    token_rows = inputs.reshape(ROUNDS, -1)
    query_rows = queries.reshape(ROUNDS, -1)
    key_rows = rotated_keys.reshape(ROUNDS, -1)
    grad_rows = out_grad.reshape(ROUNDS, -1)
    doc_of, owner_of, rank_of = round_plan(doc_starts[0], owners[0])
    home_code = owner_of * CAP8 + rank_of
    codes = jnp.stack([rank_of * LANES + owner_of, home_code])
    slot_ids = jnp.arange(CAP8, dtype=jnp.int32)
    mine = (owner_of[None, :] == own_lane) & (rank_of[None, :] == slot_ids[:, None])
    slot_doc = jnp.sum(jnp.where(mine, doc_of[None, :] + 1, 0), axis=1) - 1
    pick = (jnp.arange(KEYS, dtype=jnp.int32)[:, None] == home_code[None, :]).astype(BF)

    def place(rows):
        return jnp.dot(pick, rows, preferred_element_type=F32).astype(BF).reshape(LANES, CAP8, -1)

    def collect(slots):
        return lax.dot_general(
            pick, slots.reshape(KEYS, -1), (((0,), (0,)), ((), ())), preferred_element_type=F32
        ).astype(BF)

    x, core, zl, y = (lax.axis_index(name) for name in ("x", "core", "zl", "y"))
    steps = jnp.arange(4, dtype=jnp.int32)
    where = jnp.concatenate([(x - steps) % 4, core[None]])
    peers = (y - steps) % 4
    peer = zl * RING + y
    sources = (peer - jnp.arange(PEERS, dtype=jnp.int32)) % PEERS

    def around(value, axis):
        return [value] + [
            lax.ppermute(value, axis, [(i, (i + k) % 4) for i in range(4)])
            for k in (1, 2, 3)
        ]

    column = exchange(jnp.broadcast_to(value_weight[None], (8,) + value_weight.shape), ("zh", "zl"))
    query_split = pack_query(codes, query_rows, key_rows)
    token_split = split_features(token_rows)
    query_split, column = lax.optimization_barrier((query_split, column))
    plane = jnp.stack(around(column, "x"))
    other = lax.ppermute(plane, "core", [(0, 1), (1, 0)])
    weight_part = weight_rows(where, plane, other).reshape(2, FEATS, -1)
    weight_parts = around(weight_part, "y")

    own = exchange(query_split, SEQ)
    grad_split = pack_grad(codes, grad_rows)
    grad_split, own = lax.optimization_barrier((grad_split, own))
    grad_own = exchange(grad_split, SEQ)
    probs = attend_probs(slot_doc, own)
    tokens = []
    for k in range(PEERS):
        piece = lax.dynamic_index_in_dim(token_split, (peer + k) % PEERS, 0, keepdims=False)
        if k:
            piece = lax.ppermute(piece, FEAT, [(i, (i + k) % PEERS) for i in range(PEERS)])
        tokens.append(piece)
    token_part = token_rows_of(sources, tokens).reshape(PEERS * ROUNDS, -1)
    values = make_values(peers, token_split, weight_parts)
    value_back = attend_value(probs, grad_own)

    both = exchange(jnp.concatenate([place(values), value_back], axis=1), SEQ)
    value_home = collect(both[:, CAP8:])
    value_all = exchange(
        jnp.broadcast_to(value_home[None], (PEERS,) + value_home.shape), FEAT
    ).reshape(PEERS * ROUNDS, -1)
    query_out, key_back = attend_query(probs, own, grad_own, both)
    input_grad = make_input(peers, value_home, weight_parts)

    weight_grad = lax.dot_general(
        token_part, value_all, (((0,), (0,)), ((), ())), preferred_element_type=F32
    ).astype(BF)
    last = exchange(jnp.concatenate([weight_grad.reshape(LANES, WROWS, -1), key_back], axis=1), SEQ)
    weight_sum = jnp.sum(last[:, :WROWS].astype(F32), axis=0)
    key_home = collect(last[:, WROWS:])

    tokens_total = ROUNDS * LANES * PEERS
    ewc_grad = weight_sum * (1.0 / math.sqrt(tokens_total)) + EWC_LAMBDA * fisher * (
        value_weight.astype(F32) - anchor
    )
    return (
        query_out.reshape(1, 1, CAP, LANES, -1),
        key_home.reshape(1, ROUNDS, 1, -1),
        input_grad.reshape(1, ROUNDS, 1, -1),
        ewc_grad,
    )


def solution(mesh):
    fine = Mesh(mesh.devices.reshape(4, 4, 2, 2, 4), ("zh", "x", "core", "zl", "y"))
    rows = P(FEAT, None, SEQ, None)
    weights = P(SEQ + FEAT, None)
    plan = P(FEAT, None)
    return jax.shard_map(
        body,
        mesh=fine,
        in_specs=(rows, rows, rows, rows, weights, weights, weights, plan, plan),
        out_specs=(P(FEAT, SEQ, None, None, None), rows, rows, weights),
        check_vma=False,
    )
```

```python
import math

import jax
import jax.numpy as jnp
from jax import lax
from jax.experimental import pallas as pl
from jax.experimental.pallas import tpu as pltpu
from jax.sharding import Mesh, PartitionSpec as P


KVH = 4
HD = 128
GROUP = 8
LANES = 32
PEERS = 8
FEATS = 512
RING = 4
FEAT = ("zl", "y")
SEQ = ("zh", "x", "core")
CAP = 6
CAP8 = 8
ROUNDS = 128
WROWS = 16
HROWS = CAP * GROUP
MROWS = HROWS + CAP8
ROWS = LANES * HROWS
KEYS = LANES * CAP8
CHUNKS = 6
CHUNK = ROWS // CHUNKS
SCORE_NEG = -1e30
EWC_LAMBDA = 4.0
SCALE = 1.0 / math.sqrt(HD)
BF = jnp.bfloat16
F32 = jnp.float32


def exchange(value, axes):
    return lax.all_to_all(value, axes, split_axis=0, concat_axis=0, tiled=True)


def round_plan(starts, owner_list):
    round_ids = jnp.arange(ROUNDS, dtype=jnp.int32)
    start_rounds = starts // LANES
    doc_of = jnp.sum((start_rounds[None, :] <= round_ids[:, None]).astype(jnp.int32), axis=1) - 1
    doc_ids = jnp.arange(starts.shape[0], dtype=jnp.int32)
    onehot = (doc_of[:, None] == doc_ids[None, :]).astype(jnp.int32)
    owner_of = jnp.sum(onehot * owner_list[None, :], axis=1)
    earlier = (owner_of[:, None] == owner_of[None, :]) & (round_ids[None, :] < round_ids[:, None])
    rank_of = jnp.sum(earlier.astype(jnp.int32), axis=1)
    return doc_of, owner_of, rank_of


def pick_rows(code, count):
    slots = lax.broadcasted_iota(jnp.int32, (count, ROUNDS), 0)
    return (slots == code).astype(F32).astype(BF)


def spread_heads(code, x_ref, acc_ref):
    rows = jnp.dot(pick_rows(code, CAP * LANES), x_ref[...], preferred_element_type=F32)
    for g in range(GROUP):
        for s in range(CAP):
            acc_ref[pl.ds(s * GROUP + g, LANES, stride=HROWS), :] = rows[
                s * LANES : (s + 1) * LANES, g * HD : (g + 1) * HD
            ]
    return acc_ref[...].astype(BF).reshape(LANES, HROWS, HD)


def pack_grad_kernel(code_ref, g_ref, out_ref, acc_ref):
    out_ref[:, 0] = spread_heads(code_ref[0:1, :], g_ref, acc_ref)


def pack_query_kernel(code_ref, q_ref, k_ref, out_ref, acc_ref):
    out_ref[:, 0, 0:HROWS] = spread_heads(code_ref[0:1, :], q_ref, acc_ref)
    keys = jnp.dot(pick_rows(code_ref[1:2, :], KEYS), k_ref[...], preferred_element_type=F32)
    out_ref[:, 0, HROWS:] = keys.reshape(LANES, CAP8, HD).astype(BF)


def code_spec():
    return pl.BlockSpec((2, ROUNDS), lambda h: (0, 0))


def head_spec(rows):
    return pl.BlockSpec((LANES, 1, rows, HD), lambda h: (0, h, 0, 0))


def key_spec():
    return pl.BlockSpec((LANES, CAP8, HD), lambda h: (0, 0, h))


def probs_spec():
    return pl.BlockSpec((1, ROWS, KEYS), lambda h: (h, 0, 0))


def turned_spec():
    return pl.BlockSpec((1, KEYS, ROWS), lambda h: (h, 0, 0))


def pack_query(codes, queries, keys):
    return pl.pallas_call(
        pack_query_kernel,
        grid=(KVH,),
        in_specs=[
            code_spec(),
            pl.BlockSpec((ROUNDS, GROUP * HD), lambda h: (0, h)),
            pl.BlockSpec((ROUNDS, HD), lambda h: (0, h)),
        ],
        out_specs=head_spec(MROWS),
        out_shape=jax.ShapeDtypeStruct((LANES, KVH, MROWS, HD), BF),
        scratch_shapes=[pltpu.VMEM((ROWS, HD), F32)],
        name="pack_query",
    )(codes, queries, keys)


def pack_grad(codes, grads):
    return pl.pallas_call(
        pack_grad_kernel,
        grid=(KVH,),
        in_specs=[code_spec(), pl.BlockSpec((ROUNDS, GROUP * HD), lambda h: (0, h))],
        out_specs=head_spec(HROWS),
        out_shape=jax.ShapeDtypeStruct((LANES, KVH, HROWS, HD), BF),
        scratch_shapes=[pltpu.VMEM((ROWS, HD), F32)],
        name="pack_grad",
    )(codes, grads)


def mix_matrix(turned):
    a = lax.broadcasted_iota(jnp.int32, (1024, 1024), 1 if turned else 0)
    b = lax.broadcasted_iota(jnp.int32, (1024, 1024), 0 if turned else 1)
    target = ((a >> 4) & 7) * 128 + (a >> 7) * 16 + (a & 15)
    return (target == b).astype(F32).astype(BF)


def split_kernel(x_ref, out_ref, mix_ref):
    @pl.when(pl.program_id(0) == 0)
    def _():
        mix_ref[...] = mix_matrix(False)

    mixed = jnp.dot(x_ref[...], mix_ref[...], preferred_element_type=F32)
    for f in range(PEERS):
        out_ref[f] = mixed[:, f * 128 : (f + 1) * 128].astype(BF)


def split_features(rows):
    return pl.pallas_call(
        split_kernel,
        grid=(4,),
        in_specs=[pl.BlockSpec((ROUNDS, 1024), lambda q: (0, q))],
        out_specs=pl.BlockSpec((PEERS, ROUNDS, 128), lambda q: (0, 0, q)),
        out_shape=jax.ShapeDtypeStruct((PEERS, ROUNDS, FEATS), BF),
        scratch_shapes=[pltpu.VMEM((1024, 1024), BF)],
        name="split_features",
    )(rows)


def smem():
    return pl.BlockSpec(memory_space=pltpu.SMEM)


def weight_kernel(where_ref, same_ref, other_ref, out_ref):
    core = where_ref[4]
    for x in range(4):
        for z in range(8):
            spot = (z // 2) * 8 + where_ref[x] * 2
            out_ref[z % 2, spot + core] = same_ref[x, z]
            out_ref[z % 2, spot + 1 - core] = other_ref[x, z]


def weight_rows(where, same, other):
    return pl.pallas_call(
        weight_kernel,
        in_specs=[smem()] + [pl.BlockSpec(memory_space=pltpu.VMEM)] * 2,
        out_specs=pl.BlockSpec(memory_space=pltpu.VMEM),
        out_shape=jax.ShapeDtypeStruct((2, LANES, WROWS, KVH * HD), BF),
        name="weight_rows",
    )(where, same, other)


def partial_kernel(w_ref, *refs):
    parts, outs = refs[:RING], refs[RING:]
    for part, out in zip(parts, outs):
        total = jnp.dot(part[0], w_ref[0], preferred_element_type=F32)
        total = total + jnp.dot(part[1], w_ref[1], preferred_element_type=F32)
        out[...] = total.astype(BF)


def partial_values(weight, parts):
    whole = pl.BlockSpec(memory_space=pltpu.VMEM)
    return pl.pallas_call(
        partial_kernel,
        in_specs=[whole] * (1 + RING),
        out_specs=[whole] * RING,
        out_shape=[jax.ShapeDtypeStruct((ROUNDS, KVH * HD), BF)] * RING,
        name="partial_values",
    )(weight, *parts)


def input_kernel(peer_ref, dv_ref, *refs):
    out_ref, mix_ref, row_ref = refs[RING:]

    @pl.when(pl.program_id(0) == 0)
    def _():
        mix_ref[...] = mix_matrix(True)

    for j in range(RING):
        for z in range(2):
            part = lax.dot_general(
                dv_ref[...], refs[j][z], (((1,), (1,)), ((), ())), preferred_element_type=F32
            )
            lane = pl.multiple_of((z * RING + peer_ref[j]) * 128, 128)
            row_ref[:, pl.ds(lane, 128)] = part.astype(BF)
    out_ref[...] = jnp.dot(row_ref[...], mix_ref[...], preferred_element_type=F32).astype(BF)


def make_input(peers, value_home, parts):
    return pl.pallas_call(
        input_kernel,
        grid=(4,),
        in_specs=[smem(), pl.BlockSpec((ROUNDS, KVH * HD), lambda q: (0, 0))]
        + [pl.BlockSpec((2, 128, KVH * HD), lambda q: (0, q, 0))] * RING,
        out_specs=pl.BlockSpec((ROUNDS, 1024), lambda q: (0, q)),
        out_shape=jax.ShapeDtypeStruct((ROUNDS, 4096), BF),
        scratch_shapes=[pltpu.VMEM((1024, 1024), BF), pltpu.VMEM((ROUNDS, 1024), BF)],
        name="make_input",
    )(peers, value_home, *parts)


def token_kernel(source_ref, *refs):
    out_ref = refs[RING + 1]
    zl = source_ref[RING]
    for j in range(RING):
        out_ref[zl * RING + source_ref[j]] = refs[j][zl]
        out_ref[(1 - zl) * RING + source_ref[j]] = refs[RING][j]


def token_rows_of(sources, parts, crossed):
    whole = pl.BlockSpec(memory_space=pltpu.VMEM)
    return pl.pallas_call(
        token_kernel,
        in_specs=[smem()] + [whole] * (RING + 1),
        out_specs=whole,
        out_shape=jax.ShapeDtypeStruct((PEERS, ROUNDS, FEATS), BF),
        name="token_rows_of",
    )(sources, *parts, crossed)


def doc_table(slot, doc_ref):
    table = jnp.full(slot.shape, -2, jnp.int32)
    for s in range(CAP):
        table = jnp.where(slot == s, doc_ref[s], table)
    return table


def own_keys(block_ref):
    return block_ref[:, 0, HROWS:].astype(F32).reshape(KEYS, HD).astype(BF)


def probs_kernel(doc_ref, own_ref, p_ref, turned_ref, bias_ref):
    @pl.when(pl.program_id(0) == 0)
    def _():
        shape = (LANES, HROWS, KEYS)
        q_lane = lax.broadcasted_iota(jnp.int32, shape, 0)
        q_slot = lax.broadcasted_iota(jnp.int32, shape, 1) >> 3
        key = lax.broadcasted_iota(jnp.int32, shape, 2)
        k_lane = key >> 3
        k_slot = key & 7
        seen = (doc_table(q_slot, doc_ref) == doc_table(k_slot, doc_ref)) & (
            k_slot * LANES + k_lane <= q_slot * LANES + q_lane
        )
        bias_ref[...] = jnp.where(seen, 0.0, SCORE_NEG).astype(F32).reshape(ROWS, KEYS)

    query = own_ref[:, 0, 0:HROWS].reshape(ROWS, HD)
    keys = own_keys(own_ref)
    for c in range(CHUNKS):
        rows = slice(c * CHUNK, (c + 1) * CHUNK)
        scores = lax.dot_general(
            query[rows], keys, (((1,), (1,)), ((), ())), preferred_element_type=F32
        )
        scores = scores * SCALE + bias_ref[rows, :]
        peak = jnp.max(scores, axis=1, keepdims=True)
        weight = jnp.exp(scores - peak)
        total = jnp.sum(weight, axis=1, keepdims=True)
        probs = weight * (1.0 / total)
        p_ref[0, rows, :] = probs.astype(BF)
        turned_ref[0, :, rows] = probs.T.astype(BF)


def attend_probs(slot_doc, own):
    return pl.pallas_call(
        probs_kernel,
        grid=(KVH,),
        in_specs=[pl.BlockSpec(memory_space=pltpu.SMEM), head_spec(MROWS)],
        out_specs=(probs_spec(), turned_spec()),
        out_shape=(
            jax.ShapeDtypeStruct((KVH, ROWS, KEYS), BF),
            jax.ShapeDtypeStruct((KVH, KEYS, ROWS), BF),
        ),
        scratch_shapes=[pltpu.VMEM((ROWS, KEYS), F32)],
        name="attend_probs",
    )(slot_doc, own)


def value_kernel(p_ref, g_ref, v_ref, out_ref):
    grad = g_ref[...].reshape(ROWS, HD)
    value_grad = jnp.dot(p_ref[0], grad, preferred_element_type=F32).reshape(LANES, CAP8, HD)
    out_ref[...] = jnp.concatenate([v_ref[...].astype(F32), value_grad], axis=1).astype(BF)


def attend_value(turned, grad, values):
    return pl.pallas_call(
        value_kernel,
        grid=(KVH,),
        in_specs=[turned_spec(), head_spec(HROWS), key_spec()],
        out_specs=pl.BlockSpec((LANES, 2 * CAP8, HD), lambda h: (0, 0, h)),
        out_shape=jax.ShapeDtypeStruct((LANES, 2 * CAP8, KVH * HD), BF),
        name="attend_value",
    )(turned, grad, values)


def query_kernel(p_ref, own_ref, g_ref, v_ref, dq_ref, dk_ref, ds_ref, acc_ref):
    query = own_ref[:, 0, 0:HROWS].reshape(ROWS, HD)
    keys = own_keys(own_ref)
    grad = g_ref[...].reshape(ROWS, HD)
    values = v_ref[...].astype(F32).reshape(KEYS, HD).astype(BF)
    for c in range(CHUNKS):
        rows = slice(c * CHUNK, (c + 1) * CHUNK)
        probs = p_ref[0, rows, :]
        grad_c = grad[rows]
        attn = jnp.dot(probs, values, preferred_element_type=F32).astype(BF)
        delta = jnp.sum(grad_c.astype(F32) * attn.astype(F32), axis=1, keepdims=True)
        dprobs = lax.dot_general(
            grad_c, values, (((1,), (1,)), ((), ())), preferred_element_type=F32
        )
        dscores = (probs.astype(F32) * (dprobs - delta) * SCALE).astype(BF)
        ds_ref[rows, :] = dscores
        acc_ref[rows, :] = jnp.dot(dscores, keys, preferred_element_type=F32)
    for g in range(GROUP):
        for s in range(CAP):
            dq_ref[s, :, g * HD : (g + 1) * HD] = acc_ref[
                pl.ds(s * GROUP + g, LANES, stride=HROWS), :
            ].astype(BF)
    turned = lax.dot_general(
        query, ds_ref[...], (((0,), (0,)), ((), ())), preferred_element_type=F32
    )
    dk_ref[...] = turned.T.astype(BF).reshape(LANES, CAP8, HD)


def attend_query(probs, own, grad, values):
    return pl.pallas_call(
        query_kernel,
        grid=(KVH,),
        in_specs=[probs_spec(), head_spec(MROWS), head_spec(HROWS), key_spec()],
        out_specs=(pl.BlockSpec((CAP, LANES, GROUP * HD), lambda h: (0, 0, h)), key_spec()),
        out_shape=(
            jax.ShapeDtypeStruct((CAP, LANES, KVH * GROUP * HD), BF),
            jax.ShapeDtypeStruct((LANES, CAP8, KVH * HD), BF),
        ),
        scratch_shapes=[pltpu.VMEM((ROWS, KEYS), BF), pltpu.VMEM((ROWS, HD), F32)],
        name="attend_query",
    )(probs, own, grad, values)


def body(inputs, queries, rotated_keys, out_grad, value_weight, fisher, anchor, doc_starts, owners):
    own_lane = lax.axis_index(SEQ)
    token_rows = inputs.reshape(ROUNDS, -1)
    query_rows = queries.reshape(ROUNDS, -1)
    key_rows = rotated_keys.reshape(ROUNDS, -1)
    grad_rows = out_grad.reshape(ROUNDS, -1)
    doc_of, owner_of, rank_of = round_plan(doc_starts[0], owners[0])
    home_code = owner_of * CAP8 + rank_of
    codes = jnp.stack([rank_of * LANES + owner_of, home_code])
    slot_ids = jnp.arange(CAP8, dtype=jnp.int32)
    mine = (owner_of[None, :] == own_lane) & (rank_of[None, :] == slot_ids[:, None])
    slot_doc = jnp.sum(jnp.where(mine, doc_of[None, :] + 1, 0), axis=1) - 1
    pick = (jnp.arange(KEYS, dtype=jnp.int32)[:, None] == home_code[None, :]).astype(BF)

    def place(rows):
        return jnp.dot(pick, rows, preferred_element_type=F32).astype(BF).reshape(LANES, CAP8, -1)

    def collect(slots):
        return lax.dot_general(
            pick, slots.reshape(KEYS, -1), (((0,), (0,)), ((), ())), preferred_element_type=F32
        ).astype(BF)

    x, core, zl, y = (lax.axis_index(name) for name in ("x", "core", "zl", "y"))
    steps = jnp.arange(4, dtype=jnp.int32)
    where = jnp.concatenate([(x - steps) % 4, core[None]])
    peers = (y - steps) % 4

    def around(value, axis):
        return [value] + [
            lax.ppermute(value, axis, [(i, (i + k) % 4) for i in range(4)])
            for k in (1, 2, 3)
        ]

    column = exchange(jnp.broadcast_to(value_weight[None], (8,) + value_weight.shape), ("zh", "zl"))
    query_split = pack_query(codes, query_rows, key_rows)
    token_split = split_features(token_rows)
    query_split, column = lax.optimization_barrier((query_split, column))
    plane = jnp.stack(around(column, "x"))
    other = lax.ppermute(plane, "core", [(0, 1), (1, 0)])
    weight_part = weight_rows(where, plane, other).reshape(2, FEATS, -1)
    halves = token_split.reshape(2, RING, ROUNDS, FEATS)
    tokens = []
    for k in range(RING):
        piece = lax.dynamic_index_in_dim(halves, (y + k) % RING, 1, keepdims=False)
        if k:
            piece = lax.ppermute(piece, "y", [(i, (i + k) % RING) for i in range(RING)])
        tokens.append(piece)
    shares = partial_values(weight_part, tokens)
    values = shares[0].astype(F32)
    for k in (1, 2, 3):
        share = lax.ppermute(shares[k], "y", [(i, (i - k) % RING) for i in range(RING)])
        values = values + share.astype(F32)
    values = values.astype(BF)
    weight_parts = around(weight_part, "y")

    own = exchange(query_split, SEQ)
    grad_split = pack_grad(codes, grad_rows)
    grad_split, own = lax.optimization_barrier((grad_split, own))
    grad_own = exchange(grad_split, SEQ)
    probs, turned = attend_probs(slot_doc, own)
    crossed = jnp.stack(
        [lax.dynamic_index_in_dim(part, 1 - zl, 0, keepdims=False) for part in tokens]
    )
    crossed = lax.ppermute(crossed, "zl", [(0, 1), (1, 0)])
    token_part = token_rows_of(
        jnp.concatenate([peers, zl[None]]), tokens, crossed
    ).reshape(PEERS * ROUNDS, -1)

    both = exchange(attend_value(turned, grad_own, place(values)), SEQ)
    value_home = collect(both[:, CAP8:])
    value_all = exchange(
        jnp.broadcast_to(value_home[None], (PEERS,) + value_home.shape), FEAT
    ).reshape(PEERS * ROUNDS, -1)
    query_out, key_back = attend_query(probs, own, grad_own, both)
    input_grad = make_input(peers, value_home, weight_parts)

    weight_grad = lax.dot_general(
        token_part, value_all, (((0,), (0,)), ((), ())), preferred_element_type=F32
    ).astype(BF)
    last = exchange(jnp.concatenate([weight_grad.reshape(LANES, WROWS, -1), key_back], axis=1), SEQ)
    weight_sum = jnp.sum(last[:, :WROWS].astype(F32), axis=0)
    key_home = collect(last[:, WROWS:])

    tokens_total = ROUNDS * LANES * PEERS
    ewc_grad = weight_sum * (1.0 / math.sqrt(tokens_total)) + EWC_LAMBDA * fisher * (
        value_weight.astype(F32) - anchor
    )
    return (
        query_out.reshape(1, 1, CAP, LANES, -1),
        key_home.reshape(1, ROUNDS, 1, -1),
        input_grad.reshape(1, ROUNDS, 1, -1),
        ewc_grad,
    )


def solution(mesh):
    fine = Mesh(mesh.devices.reshape(4, 4, 2, 2, 4), ("zh", "x", "core", "zl", "y"))
    rows = P(FEAT, None, SEQ, None)
    weights = P(SEQ + FEAT, None)
    plan = P(FEAT, None)
    return jax.shard_map(
        body,
        mesh=fine,
        in_specs=(rows, rows, rows, rows, weights, weights, weights, plan, plan),
        out_specs=(P(FEAT, SEQ, None, None, None), rows, rows, weights),
        check_vma=False,
    )
```

```python
import math

import jax
import jax.numpy as jnp
from jax import lax
from jax.experimental import pallas as pl
from jax.experimental.pallas import tpu as pltpu
from jax.sharding import Mesh, PartitionSpec as P


KVH = 4
HD = 128
GROUP = 8
LANES = 32
PEERS = 8
FEATS = 512
RING = 4
FEAT = ("zl", "y")
SEQ = ("zh", "x", "core")
CAP = 6
CAP8 = 8
ROUNDS = 128
WROWS = 16
HROWS = CAP * GROUP
MROWS = HROWS + CAP8
ROWS = LANES * HROWS
KEYS = LANES * CAP8
CHUNKS = 6
CHUNK = ROWS // CHUNKS
SCORE_NEG = -1e30
EWC_LAMBDA = 4.0
SCALE = 1.0 / math.sqrt(HD)
BF = jnp.bfloat16
F32 = jnp.float32


def exchange(value, axes):
    return lax.all_to_all(value, axes, split_axis=0, concat_axis=0, tiled=True)


def round_plan(starts, owner_list):
    round_ids = jnp.arange(ROUNDS, dtype=jnp.int32)
    start_rounds = starts // LANES
    doc_of = jnp.sum((start_rounds[None, :] <= round_ids[:, None]).astype(jnp.int32), axis=1) - 1
    doc_ids = jnp.arange(starts.shape[0], dtype=jnp.int32)
    onehot = (doc_of[:, None] == doc_ids[None, :]).astype(jnp.int32)
    owner_of = jnp.sum(onehot * owner_list[None, :], axis=1)
    earlier = (owner_of[:, None] == owner_of[None, :]) & (round_ids[None, :] < round_ids[:, None])
    rank_of = jnp.sum(earlier.astype(jnp.int32), axis=1)
    return doc_of, owner_of, rank_of


def pick_rows(code, count):
    slots = lax.broadcasted_iota(jnp.int32, (count, ROUNDS), 0)
    return (slots == code).astype(F32).astype(BF)


def spread_heads(code, x_ref, acc_ref):
    rows = jnp.dot(pick_rows(code, CAP * LANES), x_ref[...], preferred_element_type=F32)
    for g in range(GROUP):
        for s in range(CAP):
            acc_ref[pl.ds(s * GROUP + g, LANES, stride=HROWS), :] = rows[
                s * LANES : (s + 1) * LANES, g * HD : (g + 1) * HD
            ]
    return acc_ref[...].astype(BF).reshape(LANES, HROWS, HD)


def pack_grad_kernel(code_ref, g_ref, out_ref, acc_ref):
    out_ref[:, 0] = spread_heads(code_ref[0:1, :], g_ref, acc_ref)


def pack_query_kernel(code_ref, q_ref, k_ref, out_ref, acc_ref):
    out_ref[:, 0, 0:HROWS] = spread_heads(code_ref[0:1, :], q_ref, acc_ref)
    keys = jnp.dot(pick_rows(code_ref[1:2, :], KEYS), k_ref[...], preferred_element_type=F32)
    out_ref[:, 0, HROWS:] = keys.reshape(LANES, CAP8, HD).astype(BF)


def code_spec():
    return pl.BlockSpec((2, ROUNDS), lambda h: (0, 0))


def head_spec(rows):
    return pl.BlockSpec((LANES, 1, rows, HD), lambda h: (0, h, 0, 0))


def key_spec():
    return pl.BlockSpec((LANES, CAP8, HD), lambda h: (0, 0, h))


def probs_spec():
    return pl.BlockSpec((1, ROWS, KEYS), lambda h: (h, 0, 0))


def turned_spec():
    return pl.BlockSpec((1, KEYS, ROWS), lambda h: (h, 0, 0))


def pack_query(codes, queries, keys):
    return pl.pallas_call(
        pack_query_kernel,
        grid=(KVH,),
        in_specs=[
            code_spec(),
            pl.BlockSpec((ROUNDS, GROUP * HD), lambda h: (0, h)),
            pl.BlockSpec((ROUNDS, HD), lambda h: (0, h)),
        ],
        out_specs=head_spec(MROWS),
        out_shape=jax.ShapeDtypeStruct((LANES, KVH, MROWS, HD), BF),
        scratch_shapes=[pltpu.VMEM((ROWS, HD), F32)],
        name="pack_query",
    )(codes, queries, keys)


def pack_grad(codes, grads):
    return pl.pallas_call(
        pack_grad_kernel,
        grid=(KVH,),
        in_specs=[code_spec(), pl.BlockSpec((ROUNDS, GROUP * HD), lambda h: (0, h))],
        out_specs=head_spec(HROWS),
        out_shape=jax.ShapeDtypeStruct((LANES, KVH, HROWS, HD), BF),
        scratch_shapes=[pltpu.VMEM((ROWS, HD), F32)],
        name="pack_grad",
    )(codes, grads)


def mix_matrix(turned):
    a = lax.broadcasted_iota(jnp.int32, (1024, 1024), 1 if turned else 0)
    b = lax.broadcasted_iota(jnp.int32, (1024, 1024), 0 if turned else 1)
    target = ((a >> 4) & 7) * 128 + (a >> 7) * 16 + (a & 15)
    return (target == b).astype(F32).astype(BF)


def split_kernel(x_ref, out_ref, mix_ref):
    @pl.when(pl.program_id(0) == 0)
    def _():
        mix_ref[...] = mix_matrix(False)

    mixed = jnp.dot(x_ref[...], mix_ref[...], preferred_element_type=F32)
    for f in range(PEERS):
        out_ref[f] = mixed[:, f * 128 : (f + 1) * 128].astype(BF)


def split_features(rows):
    return pl.pallas_call(
        split_kernel,
        grid=(4,),
        in_specs=[pl.BlockSpec((ROUNDS, 1024), lambda q: (0, q))],
        out_specs=pl.BlockSpec((PEERS, ROUNDS, 128), lambda q: (0, 0, q)),
        out_shape=jax.ShapeDtypeStruct((PEERS, ROUNDS, FEATS), BF),
        scratch_shapes=[pltpu.VMEM((1024, 1024), BF)],
        name="split_features",
    )(rows)


def smem():
    return pl.BlockSpec(memory_space=pltpu.SMEM)


def weight_kernel(where_ref, same_ref, other_ref, out_ref):
    core = where_ref[4]
    for x in range(4):
        for z in range(8):
            place = where_ref[5 + z]
            spot = (place >> 1) * 8 + where_ref[x] * 2
            out_ref[place & 1, spot + core] = same_ref[x, z]
            out_ref[place & 1, spot + 1 - core] = other_ref[x, z]


def weight_rows(where, same, other):
    return pl.pallas_call(
        weight_kernel,
        in_specs=[smem()] + [pl.BlockSpec(memory_space=pltpu.VMEM)] * 2,
        out_specs=pl.BlockSpec(memory_space=pltpu.VMEM),
        out_shape=jax.ShapeDtypeStruct((2, LANES, WROWS, KVH * HD), BF),
        name="weight_rows",
    )(where, same, other)


def partial_kernel(w_ref, *refs):
    parts, outs = refs[:RING], refs[RING:]
    for part, out in zip(parts, outs):
        total = jnp.dot(part[0], w_ref[0], preferred_element_type=F32)
        total = total + jnp.dot(part[1], w_ref[1], preferred_element_type=F32)
        out[...] = total.astype(BF)


def partial_values(weight, parts):
    whole = pl.BlockSpec(memory_space=pltpu.VMEM)
    return pl.pallas_call(
        partial_kernel,
        in_specs=[whole] * (1 + RING),
        out_specs=[whole] * RING,
        out_shape=[jax.ShapeDtypeStruct((ROUNDS, KVH * HD), BF)] * RING,
        name="partial_values",
    )(weight, *parts)


def input_kernel(peer_ref, dv_ref, *refs):
    out_ref, mix_ref, row_ref = refs[RING:]

    @pl.when(pl.program_id(0) == 0)
    def _():
        mix_ref[...] = mix_matrix(True)

    for j in range(RING):
        for z in range(2):
            part = lax.dot_general(
                dv_ref[...], refs[j][z], (((1,), (1,)), ((), ())), preferred_element_type=F32
            )
            lane = pl.multiple_of((z * RING + peer_ref[j]) * 128, 128)
            row_ref[:, pl.ds(lane, 128)] = part.astype(BF)
    out_ref[...] = jnp.dot(row_ref[...], mix_ref[...], preferred_element_type=F32).astype(BF)


def make_input(peers, value_home, parts):
    return pl.pallas_call(
        input_kernel,
        grid=(4,),
        in_specs=[smem(), pl.BlockSpec((ROUNDS, KVH * HD), lambda q: (0, 0))]
        + [pl.BlockSpec((2, 128, KVH * HD), lambda q: (0, q, 0))] * RING,
        out_specs=pl.BlockSpec((ROUNDS, 1024), lambda q: (0, q)),
        out_shape=jax.ShapeDtypeStruct((ROUNDS, 4096), BF),
        scratch_shapes=[pltpu.VMEM((1024, 1024), BF), pltpu.VMEM((ROUNDS, 1024), BF)],
        name="make_input",
    )(peers, value_home, *parts)


def token_kernel(source_ref, *refs):
    out_ref = refs[RING + 1]
    zl = source_ref[RING]
    for j in range(RING):
        out_ref[zl * RING + source_ref[j]] = refs[j][zl]
        out_ref[(1 - zl) * RING + source_ref[j]] = refs[RING][j]


def token_rows_of(sources, parts, crossed):
    whole = pl.BlockSpec(memory_space=pltpu.VMEM)
    return pl.pallas_call(
        token_kernel,
        in_specs=[smem()] + [whole] * (RING + 1),
        out_specs=whole,
        out_shape=jax.ShapeDtypeStruct((PEERS, ROUNDS, FEATS), BF),
        name="token_rows_of",
    )(sources, *parts, crossed)


def doc_table(slot, doc_ref):
    table = jnp.full(slot.shape, -2, jnp.int32)
    for s in range(CAP):
        table = jnp.where(slot == s, doc_ref[s], table)
    return table


def own_keys(block_ref):
    return block_ref[:, 0, HROWS:].astype(F32).reshape(KEYS, HD).astype(BF)


def probs_kernel(doc_ref, own_ref, p_ref, turned_ref, bias_ref):
    @pl.when(pl.program_id(0) == 0)
    def _():
        shape = (LANES, HROWS, KEYS)
        q_lane = lax.broadcasted_iota(jnp.int32, shape, 0)
        q_slot = lax.broadcasted_iota(jnp.int32, shape, 1) >> 3
        key = lax.broadcasted_iota(jnp.int32, shape, 2)
        k_lane = key >> 3
        k_slot = key & 7
        seen = (doc_table(q_slot, doc_ref) == doc_table(k_slot, doc_ref)) & (
            k_slot * LANES + k_lane <= q_slot * LANES + q_lane
        )
        bias_ref[...] = jnp.where(seen, 0.0, SCORE_NEG).astype(F32).reshape(ROWS, KEYS)

    query = own_ref[:, 0, 0:HROWS].reshape(ROWS, HD)
    keys = own_keys(own_ref)
    for c in range(CHUNKS):
        rows = slice(c * CHUNK, (c + 1) * CHUNK)
        scores = lax.dot_general(
            query[rows], keys, (((1,), (1,)), ((), ())), preferred_element_type=F32
        )
        scores = scores * SCALE + bias_ref[rows, :]
        peak = jnp.max(scores, axis=1, keepdims=True)
        weight = jnp.exp(scores - peak)
        total = jnp.sum(weight, axis=1, keepdims=True)
        probs = weight * (1.0 / total)
        p_ref[0, rows, :] = probs.astype(BF)
        turned_ref[0, :, rows] = probs.T.astype(BF)


def attend_probs(slot_doc, own):
    return pl.pallas_call(
        probs_kernel,
        grid=(KVH,),
        in_specs=[pl.BlockSpec(memory_space=pltpu.SMEM), head_spec(MROWS)],
        out_specs=(probs_spec(), turned_spec()),
        out_shape=(
            jax.ShapeDtypeStruct((KVH, ROWS, KEYS), BF),
            jax.ShapeDtypeStruct((KVH, KEYS, ROWS), BF),
        ),
        scratch_shapes=[pltpu.VMEM((ROWS, KEYS), F32)],
        name="attend_probs",
    )(slot_doc, own)


def value_kernel(p_ref, g_ref, v_ref, out_ref):
    grad = g_ref[...].reshape(ROWS, HD)
    value_grad = jnp.dot(p_ref[0], grad, preferred_element_type=F32).reshape(LANES, CAP8, HD)
    out_ref[...] = jnp.concatenate([v_ref[...].astype(F32), value_grad], axis=1).astype(BF)


def attend_value(turned, grad, values):
    return pl.pallas_call(
        value_kernel,
        grid=(KVH,),
        in_specs=[turned_spec(), head_spec(HROWS), key_spec()],
        out_specs=pl.BlockSpec((LANES, 2 * CAP8, HD), lambda h: (0, 0, h)),
        out_shape=jax.ShapeDtypeStruct((LANES, 2 * CAP8, KVH * HD), BF),
        name="attend_value",
    )(turned, grad, values)


def query_kernel(p_ref, own_ref, g_ref, v_ref, dq_ref, dk_ref, ds_ref, acc_ref):
    query = own_ref[:, 0, 0:HROWS].reshape(ROWS, HD)
    keys = own_keys(own_ref)
    grad = g_ref[...].reshape(ROWS, HD)
    values = v_ref[...].astype(F32).reshape(KEYS, HD).astype(BF)
    for c in range(CHUNKS):
        rows = slice(c * CHUNK, (c + 1) * CHUNK)
        probs = p_ref[0, rows, :]
        grad_c = grad[rows]
        attn = jnp.dot(probs, values, preferred_element_type=F32).astype(BF)
        delta = jnp.sum(grad_c.astype(F32) * attn.astype(F32), axis=1, keepdims=True)
        dprobs = lax.dot_general(
            grad_c, values, (((1,), (1,)), ((), ())), preferred_element_type=F32
        )
        dscores = (probs.astype(F32) * (dprobs - delta) * SCALE).astype(BF)
        ds_ref[rows, :] = dscores
        acc_ref[rows, :] = jnp.dot(dscores, keys, preferred_element_type=F32)
    for g in range(GROUP):
        for s in range(CAP):
            dq_ref[s, :, g * HD : (g + 1) * HD] = acc_ref[
                pl.ds(s * GROUP + g, LANES, stride=HROWS), :
            ].astype(BF)
    turned = lax.dot_general(
        query, ds_ref[...], (((0,), (0,)), ((), ())), preferred_element_type=F32
    )
    dk_ref[...] = turned.T.astype(BF).reshape(LANES, CAP8, HD)


def attend_query(probs, own, grad, values):
    return pl.pallas_call(
        query_kernel,
        grid=(KVH,),
        in_specs=[probs_spec(), head_spec(MROWS), head_spec(HROWS), key_spec()],
        out_specs=(pl.BlockSpec((CAP, LANES, GROUP * HD), lambda h: (0, 0, h)), key_spec()),
        out_shape=(
            jax.ShapeDtypeStruct((CAP, LANES, KVH * GROUP * HD), BF),
            jax.ShapeDtypeStruct((LANES, CAP8, KVH * HD), BF),
        ),
        scratch_shapes=[pltpu.VMEM((ROWS, KEYS), BF), pltpu.VMEM((ROWS, HD), F32)],
        name="attend_query",
    )(probs, own, grad, values)


def body(inputs, queries, rotated_keys, out_grad, value_weight, fisher, anchor, doc_starts, owners):
    own_lane = lax.axis_index(SEQ)
    token_rows = inputs.reshape(ROUNDS, -1)
    query_rows = queries.reshape(ROUNDS, -1)
    key_rows = rotated_keys.reshape(ROUNDS, -1)
    grad_rows = out_grad.reshape(ROUNDS, -1)
    doc_of, owner_of, rank_of = round_plan(doc_starts[0], owners[0])
    home_code = owner_of * CAP8 + rank_of
    codes = jnp.stack([rank_of * LANES + owner_of, home_code])
    slot_ids = jnp.arange(CAP8, dtype=jnp.int32)
    mine = (owner_of[None, :] == own_lane) & (rank_of[None, :] == slot_ids[:, None])
    slot_doc = jnp.sum(jnp.where(mine, doc_of[None, :] + 1, 0), axis=1) - 1
    pick = (jnp.arange(KEYS, dtype=jnp.int32)[:, None] == home_code[None, :]).astype(BF)

    def place(rows):
        return jnp.dot(pick, rows, preferred_element_type=F32).astype(BF).reshape(LANES, CAP8, -1)

    def collect(slots):
        return lax.dot_general(
            pick, slots.reshape(KEYS, -1), (((0,), (0,)), ((), ())), preferred_element_type=F32
        ).astype(BF)

    x, core, zl, y = (lax.axis_index(name) for name in ("x", "core", "zl", "y"))
    steps = jnp.arange(4, dtype=jnp.int32)
    zs = lax.axis_index(("zh", "zl"))
    where = jnp.concatenate([(x - steps) % 4, core[None], (zs - jnp.arange(8, dtype=jnp.int32)) % 8])
    peers = (y - steps) % 4

    def around(value, axis):
        return [value] + [
            lax.ppermute(value, axis, [(i, (i + k) % 4) for i in range(4)])
            for k in (1, 2, 3)
        ]

    ring = 8
    column = [value_weight] + [
        lax.ppermute(value_weight, ("zh", "zl"), [(i, (i + k) % ring) for i in range(ring)])
        for k in range(1, ring)
    ]
    column = jnp.stack(column)
    query_split = pack_query(codes, query_rows, key_rows)
    token_split = split_features(token_rows)
    plane = jnp.stack(around(column, "x"))
    other = lax.ppermute(plane, "core", [(0, 1), (1, 0)])
    weight_part = weight_rows(where, plane, other).reshape(2, FEATS, -1)
    halves = token_split.reshape(2, RING, ROUNDS, FEATS)
    tokens = []
    for k in range(RING):
        piece = lax.dynamic_index_in_dim(halves, (y + k) % RING, 1, keepdims=False)
        if k:
            piece = lax.ppermute(piece, "y", [(i, (i + k) % RING) for i in range(RING)])
        tokens.append(piece)
    shares = partial_values(weight_part, tokens)
    values = shares[0].astype(F32)
    for k in (1, 2, 3):
        share = lax.ppermute(shares[k], "y", [(i, (i - k) % RING) for i in range(RING)])
        values = values + share.astype(F32)
    values = values.astype(BF)
    weight_parts = around(weight_part, "y")

    own = exchange(query_split, SEQ)
    grad_split = pack_grad(codes, grad_rows)
    grad_split, own = lax.optimization_barrier((grad_split, own))
    grad_own = exchange(grad_split, SEQ)
    probs, turned = attend_probs(slot_doc, own)
    crossed = jnp.stack(
        [lax.dynamic_index_in_dim(part, 1 - zl, 0, keepdims=False) for part in tokens]
    )
    crossed = lax.ppermute(crossed, "zl", [(0, 1), (1, 0)])
    token_part = token_rows_of(
        jnp.concatenate([peers, zl[None]]), tokens, crossed
    ).reshape(PEERS * ROUNDS, -1)

    both = exchange(attend_value(turned, grad_own, place(values)), SEQ)
    value_home = collect(both[:, CAP8:])
    value_all = exchange(
        jnp.broadcast_to(value_home[None], (PEERS,) + value_home.shape), FEAT
    ).reshape(PEERS * ROUNDS, -1)
    query_out, key_back = attend_query(probs, own, grad_own, both)
    input_grad = make_input(peers, value_home, weight_parts)

    weight_grad = lax.dot_general(
        token_part, value_all, (((0,), (0,)), ((), ())), preferred_element_type=F32
    ).astype(BF)
    last = exchange(jnp.concatenate([weight_grad.reshape(LANES, WROWS, -1), key_back], axis=1), SEQ)
    weight_sum = jnp.sum(last[:, :WROWS].astype(F32), axis=0)
    key_home = collect(last[:, WROWS:])

    tokens_total = ROUNDS * LANES * PEERS
    ewc_grad = weight_sum * (1.0 / math.sqrt(tokens_total)) + EWC_LAMBDA * fisher * (
        value_weight.astype(F32) - anchor
    )
    return (
        query_out.reshape(1, 1, CAP, LANES, -1),
        key_home.reshape(1, ROUNDS, 1, -1),
        input_grad.reshape(1, ROUNDS, 1, -1),
        ewc_grad,
    )


def solution(mesh):
    fine = Mesh(mesh.devices.reshape(4, 4, 2, 2, 4), ("zh", "x", "core", "zl", "y"))
    rows = P(FEAT, None, SEQ, None)
    weights = P(SEQ + FEAT, None)
    plan = P(FEAT, None)
    return jax.shard_map(
        body,
        mesh=fine,
        in_specs=(rows, rows, rows, rows, weights, weights, weights, plan, plan),
        out_specs=(P(FEAT, SEQ, None, None, None), rows, rows, weights),
        check_vma=False,
    )
```
